128 devices in a mesh: gz: 64 (over y, z, x_lo, core), rows: 2 (over x_hi).
Axes of the slice: x: 4 (x_hi: 2, x_lo: 2; x = x_hi * 2 + x_lo), y: 4, z: 4, core: 2. Of those that a mesh axis runs over, the one named last changes fastest.
Arguments:
- unary_cost: bfloat16 [256, 8, 225, 512], P('gz', 'rows'), may hold values from -6 to 6
- descriptors: bfloat16 [256, 225, 256], P('gz'), may hold values from -0.25 to 0.25
- valid_rows: int32 [256, 8], P('gz', 'rows'), may hold values 0 or 1
- offsets: int32 [225, 2], replicated, may hold values from -7 to 7, as said below
Outputs:
- energy: float32 [256, 8, 225, 512], P('gz', 'rows')
- displacement: float32 [2, 256, 8, 512], P(None, 'gz', 'rows')
The draws below stay inside these ranges and needn't reach their ends.
Inputs may be any that keep to these rules, and one draw needn't show every extreme that they name: `offsets`: each row is a distinct pair, and every pair of whole numbers from -(7) to 7 appears once.
All inputs are finite; a program needn't handle non-finite values. No bound on the sum of `valid_rows` on one device may be relied on, other than what follows from the above.
Results may differ from the reference program's by a relative error of at most 0.0032.
Values may be sent and summed in bfloat16 or wider, within the bound.
A program may use at most 128 MiB of HBM per device.

```python
from functools import partial
import jax
import jax.numpy as jnp
from jax import lax

SIDE = 15
LABELS = 225
FEAT = 256
COLS = 512
SWEEPS = 2
SECTIONS = 256
STRIP_ROWS = 8


def draw_offsets(key, part):
    ordering = jax.random.permutation(key, SIDE * SIDE)
    centre = SIDE // 2
    return jnp.stack([ordering // SIDE - centre, ordering % SIDE - centre], axis=1).astype(jnp.int32)


def with_ends(entries, stream_key, smallest, top_value):
    longest = entries.shape.index(max(entries.shape))
    spots = []
    for shift in (0, 1):
        where = [jax.random.randint(jax.random.fold_in(stream_key, axis), (), 0, length) for axis, length in enumerate(entries.shape)]
        where[longest] = (where[longest] + shift) % entries.shape[longest]
        spots.append(tuple(where))
    return entries.at[spots[0]].set(smallest).at[spots[1]].set(top_value)


def block_levels(rng, shape, pieces, low, largest):
    loudness = 1.0
    for axis_at, blocks in pieces:
        draws = jax.random.uniform(jax.random.fold_in(jax.random.fold_in(rng, 6), axis_at), (blocks,), jnp.float32, low / len(pieces), largest / len(pieces))
        loudness = loudness * jnp.repeat(jnp.exp(draws), shape[axis_at] // blocks).reshape((-1,) + (1,) * (len(shape) - 1 - axis_at))
    return loudness


def normal_values(rng, extent, scale, most, shards=(), kind=jnp.bfloat16):
    values = jax.random.normal(rng, extent, jnp.float32) * scale
    if len(shards) > 0:
        values = block_levels(rng, extent, shards, -0.22, 0.18) * values
    return jnp.clip(values, min=-most, max=most).astype(kind)


def setup_inputs(seed: int = 0) -> dict:
    key_of = jax.random.split(jax.random.key(seed), 5)
    return {
        "unary_cost": normal_values(key_of[0], (SECTIONS, STRIP_ROWS, LABELS, COLS), 1.5, 6.0, ((0, 64), (1, 2))),
        "descriptors": jnp.clip(jax.random.uniform(key_of[1], (SECTIONS, LABELS, FEAT), jnp.float32, -0.25, 0.25) * block_levels(key_of[1], (SECTIONS, LABELS, FEAT), ((0, 64),), -0.4, 0.0), -0.25, 0.25).astype(jnp.bfloat16),
        "valid_rows": with_ends((jax.random.randint(key_of[2], (SECTIONS, STRIP_ROWS), 0, 4) < 3).astype(jnp.int32), jax.random.fold_in(key_of[2], 1), 0, 1),
        "offsets": draw_offsets(jax.random.fold_in(key_of[4], 71), 0),
    }


NEAR_WEIGHT = 1.0
FAR_WEIGHT = 0.5


def compat_table(offsets):
    coords = offsets.astype(jnp.float32)
    spread = jnp.abs(coords[:, None, 0] - coords[None, :, 0]) + jnp.abs(coords[:, None, 1] - coords[None, :, 1])
    return 0.125 * jnp.minimum(spread, 6.0)


def pair_matrix(lower_rows, upper_rows, compat, weight):
    products = jnp.einsum("saf,sbf->sab", lower_rows.astype(jnp.float32), upper_rows.astype(jnp.float32), precision=lax.Precision.HIGHEST)
    return (weight * compat + products).astype(jnp.bfloat16)


def normalize(energy):
    weights = jnp.exp(-energy)
    return (weights / jnp.sum(weights, axis=-2, keepdims=True)).astype(jnp.bfloat16)


def pick_entry(table, position):
    return lax.dynamic_index_in_dim(table, position.astype(jnp.int32), 0, keepdims=False).astype(jnp.float32)


def neighbour_section(current, section, offset):
    target = section + offset
    clipped = jnp.clip(target, 0, SECTIONS - 1).astype(jnp.int32)
    picked = lax.dynamic_index_in_dim(current, clipped, 0, keepdims=False)
    present = jnp.logical_and(target >= 0, target < SECTIONS)
    return jnp.where(present, picked, jnp.zeros_like(picked)).astype(jnp.float32)


def section_data(unary_cost, valid_rows, section):
    rows_mask = lax.dynamic_index_in_dim(valid_rows, section, 0, keepdims=False).astype(jnp.float32)
    costs = lax.dynamic_index_in_dim(unary_cost, section, 0, keepdims=False).astype(jnp.float32)
    return rows_mask[:, None, None] * costs


def first_marginal(unary_cost, valid_rows, section):
    return normalize(section_data(unary_cost, valid_rows, section))


def update(unary_cost, valid_rows, compat_half, near_costs, far_costs, current, section):
    own_marginal = lax.dynamic_index_in_dim(current, section, 0, keepdims=False)
    grid_view = own_marginal.astype(jnp.float32)
    framed = jnp.pad(grid_view, ((1, 1), (0, 0), (1, 1)))
    neighbours = framed[0:STRIP_ROWS, :, 1:COLS + 1] + framed[2:STRIP_ROWS + 2, :, 1:COLS + 1]
    neighbours = neighbours + framed[1:STRIP_ROWS + 1, :, 0:COLS] + framed[1:STRIP_ROWS + 1, :, 2:COLS + 2]
    neighbours = neighbours.astype(jnp.bfloat16).astype(jnp.float32)
    compat_wide = compat_half.astype(jnp.float32)
    in_plane = jnp.einsum("ab,rbc->rac", compat_wide, neighbours)
    above_near = jnp.einsum("ab,rbc->rac", pick_entry(near_costs, section + 2), neighbour_section(current, section, 1))
    above_far = jnp.einsum("ab,rbc->rac", pick_entry(far_costs, section + 2), neighbour_section(current, section, 2))
    below_near = jnp.einsum("ba,rbc->rac", pick_entry(near_costs, section + 1), neighbour_section(current, section, -1))
    below_far = jnp.einsum("ba,rbc->rac", pick_entry(far_costs, section), neighbour_section(current, section, -2))
    energy = section_data(unary_cost, valid_rows, section) + in_plane + above_near + above_far + below_near + below_far
    return energy, normalize(energy)


def reference(unary_cost, descriptors, valid_rows, offsets):
    compat = compat_table(offsets)
    compat_half = compat.astype(jnp.bfloat16)
    padded_desc = jnp.pad(descriptors, ((2, 2), (0, 0), (0, 0)))
    near_costs = pair_matrix(padded_desc[0:SECTIONS + 3], padded_desc[1:SECTIONS + 4], compat, NEAR_WEIGHT)
    far_costs = pair_matrix(padded_desc[0:SECTIONS + 2], padded_desc[2:SECTIONS + 4], compat, FAR_WEIGHT)
    section_ids = jnp.arange(SECTIONS, dtype=jnp.int32)
    marginal = lax.map(partial(first_marginal, unary_cost, valid_rows), section_ids)
    energy = jnp.zeros((SECTIONS, STRIP_ROWS, LABELS, COLS), jnp.float32)
    for sweep_index in range(SWEEPS):
        energy, marginal = lax.map(partial(update, unary_cost, valid_rows, compat_half, near_costs, far_costs, marginal), section_ids)
    displacement = jnp.einsum("zrac,ak->kzrc", marginal.astype(jnp.float32), offsets.astype(jnp.float32))
    return energy, displacement
```

```python
import functools

import jax
import jax.numpy as jnp
from jax import lax
from jax.experimental import pallas as pl
from jax.experimental.pallas import tpu as pltpu
from jax.sharding import PartitionSpec as P

BF = jnp.bfloat16
F32 = jnp.float32
MESH = pl.DeviceIdType.MESH
LAB = 225
FEAT = 256
COLS = 512
SKIP = frozenset()


def kernel(n, data, desc, compat_in, off_in, out, disp, x, xr, m0, m0r, p0, p0r, p1, m1, dd, dt, compat, off, s_buf, ps_buf, stage, send, recv, load, store):
    d = lax.axis_index("gz")
    h = lax.axis_index("rows")
    par = lax.rem(d, 2)
    prev = lax.rem(d + n - 1, n)
    nxt = lax.rem(d + 1, n)
    other = 1 - h
    relay_to = lax.rem(d + n - 1 + 2 * par, n)
    swap_with = d + 1 - 2 * par
    r0 = 2 - 2 * h
    r_edge = 3 - 3 * h
    below = jnp.where(d > 0, 1.0, 0.0).astype(F32)
    above = jnp.where(d < n - 1, 1.0, 0.0).astype(F32)

    def row(q):
        return q + h * (3 - 2 * q)

    barrier = pltpu.get_barrier_semaphore()
    for g in (prev, nxt):
        for k in (h, other):
            pl.semaphore_signal(barrier, inc=1, device_id=(g, k), device_id_type=MESH)
    pl.semaphore_wait(barrier, 4)

    count = [0]

    def remote(src, dst, g, k):
        i = count[0]
        count[0] += 1
        return pltpu.make_async_remote_copy(src_ref=src, dst_ref=dst, send_sem=send.at[i], recv_sem=recv.at[i], device_id=(g, k), device_id_type=MESH)

    near_up = remote(data.at[:, pl.ds(2, 2)], x.at[:, pl.ds(2, 2)], nxt, h)
    near_dn = remote(data.at[:, pl.ds(0, 2)], x.at[:, pl.ds(8, 2)], prev, h)
    desc_up = remote(desc, dd.at[pl.ds(0, 4)], nxt, other)
    desc_dn = remote(desc, dd.at[pl.ds(8, 4)], prev, other)
    corner = remote(data.at[r_edge, pl.ds(2 * par, 2)], xr.at[other, pl.ds(6 - 6 * par, 2)], relay_to, other)
    edge_up = remote(data.at[pl.ds(r0, 2), pl.ds(0, 2)], x.at[pl.ds(r0, 2), pl.ds(0, 2)], nxt, h)
    edge_dn = remote(data.at[pl.ds(r0, 2), pl.ds(2, 2)], x.at[pl.ds(r0, 2), pl.ds(10, 2)], prev, h)
    far_up = remote(data.at[pl.ds(2 - r0, 2), pl.ds(0, 2)], x.at[pl.ds(2 - r0, 2), pl.ds(0, 2)], nxt, h)
    far_dn = remote(data.at[pl.ds(2 - r0, 2), pl.ds(2, 2)], x.at[pl.ds(2 - r0, 2), pl.ds(10, 2)], prev, h)
    relay_near = remote(x.at[pl.ds(r0, 2), pl.ds(2 + 6 * par, 2)], xr.at[:, pl.ds(4 - 2 * par, 2)], relay_to, other)
    relay_far = remote(x.at[pl.ds(r0, 2), pl.ds(10 * par, 2)], xr.at[:, pl.ds(2 + 2 * par, 2)], relay_to, other)
    swap = remote(xr.at[h, pl.ds(4 - 2 * par, 2)], xr.at[h, pl.ds(6 * par, 2)], swap_with, h)

    for c in (near_up, near_dn, desc_up, desc_dn, corner, edge_up, edge_dn, far_up, far_dn):
        c.start()
    loads = [
        pltpu.make_async_copy(data, x.at[:, pl.ds(4, 4)], load.at[0]),
        pltpu.make_async_copy(desc, dd.at[pl.ds(4, 4)], load.at[1]),
        pltpu.make_async_copy(compat_in, compat, load.at[2]),
        pltpu.make_async_copy(off_in, off, load.at[3]),
    ]
    for c in loads:
        c.start()
    for c in loads:
        c.wait()

    def loop(count_, body):
        lax.fori_loop(0, count_, lambda i, c: (body(i), c)[1], 0)

    def soft_to(src, dst, flag):
        for j in range(4):
            cols = pl.ds(128 * j, 128)
            w = jnp.exp(-src[:, cols].astype(F32))
            inv = flag / jnp.sum(w, axis=0, keepdims=True)
            dst[:, cols] = (w * inv).astype(BF)

    def flag_of(e):
        return jnp.where(e < 4, below, jnp.where(e > 7, above, 1.0))

    def transpose(e):
        dt[e] = jnp.transpose(dd[e].astype(F32)).astype(BF)

    def project(e, src, dst):
        dst[...] = jnp.dot(dt[e], src[...], preferred_element_type=F32).astype(BF)

    def first(r, e):
        soft_to(x.at[r, e], m0.at[r, e], flag_of(e))
        project(e, m0.at[r, e], p0.at[r, e])

    lane = lax.broadcasted_iota(jnp.int32, (LAB, COLS), 1)

    def gather(near, far, planes, centre):
        s = near[0][...].astype(F32) + near[1][...].astype(F32)
        s = s + 0.5 * (far[0][...].astype(F32) + far[1][...].astype(F32))
        for p in planes:
            s = s + p[...].astype(F32)
        c = centre[...].astype(F32)
        s = s + jnp.where(lane > 0, pltpu.roll(c, 1, 1), 0.0)
        s = s + jnp.where(lane < COLS - 1, pltpu.roll(c, COLS - 1, 1), 0.0)
        s_buf[...] = s.astype(BF)

    def gather_p(a, b, c, g, e):
        ps_buf[...] = (a[...].astype(F32) + b[...].astype(F32) + c[...].astype(F32) + g[...].astype(F32)).astype(BF)

    def energy_of(e, dref, cols):
        v = dref[:, cols].astype(F32)
        v = v + jnp.dot(compat[...], s_buf[:, cols], preferred_element_type=F32)
        return v + jnp.dot(dd[e], ps_buf[:, cols], preferred_element_type=F32)

    def norm(v, flag):
        w = jnp.exp(-v)
        inv = flag / jnp.sum(w, axis=0, keepdims=True)
        return (w * inv).astype(BF)

    def mz(r, e):
        return m0.at[r, e]

    def sweep1(q, e, dst):
        r = row(q)
        planes = []
        if q > 0:
            planes.append(m0.at[row(q - 1), e])
        planes.append(m0.at[row(q + 1), e] if q < 3 else m0r.at[e - 2])
        gather((mz(r, e - 1), mz(r, e + 1)), (mz(r, e - 2), mz(r, e + 2)), planes, mz(r, e))
        gather_p(p0.at[r, e - 1], p0.at[r, e + 1], p0.at[r, e - 2], p0.at[r, e + 2], e)
        for j in range(2):
            cols = pl.ds(256 * j, 256)
            dst[:, cols] = norm(energy_of(e, x.at[r, e], cols), flag_of(e))

    def sweep1_rim(e):
        t = e - 2
        gather((m0r.at[t - 1], m0r.at[t + 1]), (m0r.at[t - 2], m0r.at[t + 2]), [m0.at[row(3), e], m0r.at[8 + e - 4]], m0r.at[t])
        gather_p(p0r.at[t - 1], p0r.at[t + 1], p0r.at[t - 2], p0r.at[t + 2], e)
        for j in range(2):
            cols = pl.ds(256 * j, 256)
            m0r.at[8 + e - 4][:, cols] = norm(energy_of(e, xr.at[h, t], cols), 1.0)

    def m1_at(r, e):
        return x.at[r, e]

    def copy_out(r, k):
        return pltpu.make_async_copy(stage.at[k], out.at[k, :, r, :], store.at[k])

    def sweep2(q, first_use):
        r = row(q)

        def one(k):
            e = 4 + k
            planes = []
            if q > 0:
                planes.append(m1.at[row(q - 1), k])
            planes.append(m1.at[row(q + 1), k] if q < 3 else m0r.at[8 + k])
            gather(*NEIGH(r, k), planes, m1.at[r, k])
            if not first_use:
                copy_out(r, k).wait()
            for j in range(2):
                cols = pl.ds(256 * j, 256)
                v = energy_of(e, x.at[r, e], cols)
                stage.at[k][:, cols] = v
                disp.at[k, r][:, cols] = jnp.dot(off[...], norm(v, 1.0), preferred_element_type=F32)
            copy_out(r, k).start()

        def NEIGH(r, k):
            def at(e):
                return m1.at[r, e - 4] if 4 <= e < 8 else x.at[r, e]
            e = 4 + k
            pp = [p1.at[r, t - 2] for t in (e - 1, e + 1, e - 2, e + 2)]
            gather_p(*pp, e)
            return (at(e - 1), at(e + 1)), (at(e - 2), at(e + 2))

        for k in range(4):
            one(k)

    def project1(q, e):
        r = row(q)
        project(e, x.at[r, e], p1.at[r, e - 2])

    def project1_own(q, k):
        r = row(q)
        project(4 + k, m1.at[r, k], p1.at[r, 2 + k])

    def wing(i):
        return 2 + i + 4 * lax.div(i, 2)

    def tip(i):
        return i + 8 * lax.div(i, 2)

    loop(4, lambda i: transpose(4 + i))
    loop(16, lambda i: first(lax.div(i, 4), 4 + lax.rem(i, 4)))

    near_up.wait_recv()
    near_dn.wait_recv()
    relay_near.start()
    desc_up.wait_recv()
    desc_dn.wait_recv()
    loop(8, lambda i: transpose(i + 4 * lax.div(i, 4)))
    loop(16, lambda i: first(lax.div(i, 4), wing(lax.rem(i, 4))))
    for q in range(3):
        loop(4, lambda i: sweep1(q, 4 + i, m1.at[row(q), i]))
        loop(4, lambda i: project1_own(q, i))

    edge_up.wait_recv()
    edge_dn.wait_recv()
    relay_far.start()
    loop(8, lambda i: first(row(2 + lax.div(i, 4)), tip(lax.rem(i, 4))))

    corner.wait_recv()
    relay_near.wait()
    loop(4, lambda i: sweep1(2, wing(i), x.at[row(2), wing(i)]))
    loop(4, lambda i: project1(2, wing(i)))
    relay_far.wait_recv()
    swap.start()
    swap.wait_recv()

    def rim(t):
        soft_to(xr.at[h, t], m0r.at[t], flag_of(t + 2))
        project(t + 2, m0r.at[t], p0r.at[t])

    loop(8, rim)
    loop(4, lambda i: soft_to(xr.at[other, i + 2], m0r.at[8 + i], 1.0))
    loop(4, lambda i: sweep1_rim(4 + i))
    loop(4, lambda i: sweep1(3, 4 + i, m1.at[row(3), i]))
    loop(4, lambda i: project1_own(3, i))
    relay_far.wait_send()
    loop(4, lambda i: sweep1(3, wing(i), x.at[row(3), wing(i)]))
    loop(4, lambda i: project1(3, wing(i)))
    sweep2(3, True)
    sweep2(2, False)

    far_up.wait_recv()
    far_dn.wait_recv()
    loop(8, lambda i: first(row(lax.div(i, 4)), tip(lax.rem(i, 4))))
    for q in (1, 0):
        loop(4, lambda i: sweep1(q, wing(i), x.at[row(q), wing(i)]))
        loop(4, lambda i: project1(q, wing(i)))
        sweep2(q, False)
    for k in range(4):
        copy_out(row(0), k).wait()
    for c in (near_up, near_dn, desc_up, desc_dn, corner, edge_up, edge_dn, far_up, far_dn, swap):
        c.wait_send()


def on_device(n, unary_cost, descriptors, valid_rows, offsets):
    data = jnp.transpose(unary_cost, (1, 0, 2, 3)) * valid_rows.astype(BF).T[:, :, None, None]
    co = offsets.astype(F32)
    spread = jnp.abs(co[:, None, 0] - co[None, :, 0]) + jnp.abs(co[:, None, 1] - co[None, :, 1])
    compat = (0.125 * jnp.minimum(spread, 6.0)).astype(BF)
    off8 = jnp.concatenate([offsets.T, jnp.zeros((6, LAB), offsets.dtype)], axis=0).astype(BF)
    hbm = pl.BlockSpec(memory_space=pl.ANY)
    e, disp = pl.pallas_call(
        functools.partial(kernel, n),
        in_specs=[hbm] * 4,
        out_specs=[hbm, pl.BlockSpec(memory_space=pltpu.VMEM)],
        out_shape=[jax.ShapeDtypeStruct((4, LAB, 4, COLS), F32), jax.ShapeDtypeStruct((4, 4, 8, COLS), F32)],
        scratch_shapes=[
            pltpu.VMEM((4, 12, LAB, COLS), BF),
            pltpu.VMEM((2, 8, LAB, COLS), BF),
            pltpu.VMEM((4, 12, LAB, COLS), BF),
            pltpu.VMEM((12, LAB, COLS), BF),
            pltpu.VMEM((4, 12, FEAT, COLS), BF),
            pltpu.VMEM((8, FEAT, COLS), BF),
            pltpu.VMEM((4, 8, FEAT, COLS), BF),
            pltpu.VMEM((4, 4, LAB, COLS), BF),
            pltpu.VMEM((12, LAB, FEAT), BF),
            pltpu.VMEM((12, FEAT, LAB), BF),
            pltpu.VMEM((LAB, LAB), BF),
            pltpu.VMEM((8, LAB), BF),
            pltpu.VMEM((LAB, COLS), BF),
            pltpu.VMEM((FEAT, COLS), BF),
            pltpu.VMEM((4, LAB, COLS), F32),
            pltpu.SemaphoreType.DMA((12,)),
            pltpu.SemaphoreType.DMA((12,)),
            pltpu.SemaphoreType.DMA((4,)),
            pltpu.SemaphoreType.DMA((4,)),
        ],
        compiler_params=pltpu.CompilerParams(collective_id=0, has_side_effects=True, vmem_limit_bytes=67043328),
        name="mega",
    )(data, descriptors, compat, off8)
    return jnp.transpose(e, (0, 2, 1, 3)), jnp.transpose(disp[:, :, 0:2], (2, 0, 1, 3))


def solution(mesh):
    in_specs = (P("gz", "rows", None, None), P("gz", None, None), P("gz", "rows"), P())
    out_specs = (P("gz", "rows", None, None), P(None, "gz", "rows", None))
    return jax.shard_map(functools.partial(on_device, mesh.shape["gz"]), mesh=mesh, in_specs=in_specs, out_specs=out_specs, check_vma=False)
```

```python
import functools

import jax
import jax.numpy as jnp
from jax import lax
from jax.experimental import pallas as pl
from jax.experimental.pallas import tpu as pltpu
from jax.sharding import PartitionSpec as P

BF = jnp.bfloat16
F32 = jnp.float32
MESH = pl.DeviceIdType.MESH
LAB = 225
FEAT = 256
COLS = 512


def kernel(n, data, desc, compat_in, off_in, out, disp, x, xr, m0, m0r, p0, p0r, p1, m1, dd, dt, compat, off, s0, s1, ps0, ps1, stage, send, recv, load, store):
    d = lax.axis_index("gz")
    h = lax.axis_index("rows")
    par = lax.rem(d, 2)
    prev = lax.rem(d + n - 1, n)
    nxt = lax.rem(d + 1, n)
    other = 1 - h
    relay_to = lax.rem(d + n - 1 + 2 * par, n)
    swap_with = d + 1 - 2 * par
    r0 = 2 - 2 * h
    s_bufs = (s0, s1)
    ps_bufs = (ps0, ps1)
    r_edge = 3 - 3 * h
    below = jnp.where(d > 0, 1.0, 0.0).astype(F32)
    above = jnp.where(d < n - 1, 1.0, 0.0).astype(F32)

    def row(q):
        return q + h * (3 - 2 * q)

    barrier = pltpu.get_barrier_semaphore()
    for g in (prev, nxt):
        for k in (h, other):
            pl.semaphore_signal(barrier, inc=1, device_id=(g, k), device_id_type=MESH)
    pl.semaphore_wait(barrier, 4)

    count = [0]

    def remote(src, dst, g, k):
        i = count[0]
        count[0] += 1
        return pltpu.make_async_remote_copy(src_ref=src, dst_ref=dst, send_sem=send.at[i], recv_sem=recv.at[i], device_id=(g, k), device_id_type=MESH)

    def blocks(rows, up_s, up_e, dn_s, dn_e):
        return (
            remote(data.at[rows, pl.ds(up_s, 2)], x.at[rows, pl.ds(up_e, 2)], nxt, h),
            remote(data.at[rows, pl.ds(dn_s, 2)], x.at[rows, pl.ds(dn_e, 2)], prev, h),
        )

    edge_rows = pl.ds(r0, 2)
    near_edge = blocks(edge_rows, 2, 2, 0, 8)
    far_edge = blocks(edge_rows, 0, 0, 2, 10)
    near_rest = blocks(pl.ds(2 - r0, 2), 2, 2, 0, 8)
    far_one = blocks(pl.ds(row(1), 1), 0, 0, 2, 10)
    far_zero = blocks(pl.ds(row(0), 1), 0, 0, 2, 10)
    desc_up = remote(desc, dd.at[pl.ds(0, 4)], nxt, jnp.where(par == 0, h, other))
    desc_dn = remote(desc, dd.at[pl.ds(8, 4)], prev, jnp.where(par == 0, other, h))
    corner = remote(data.at[r_edge, pl.ds(2 * par, 2)], xr.at[other, pl.ds(6 - 6 * par, 2)], relay_to, other)
    relay_near = remote(x.at[edge_rows, pl.ds(2 + 6 * par, 2)], xr.at[:, pl.ds(4 - 2 * par, 2)], relay_to, other)
    relay_far = remote(x.at[edge_rows, pl.ds(10 * par, 2)], xr.at[:, pl.ds(2 + 2 * par, 2)], relay_to, other)
    swap = remote(xr.at[h, pl.ds(4 - 2 * par, 2)], xr.at[h, pl.ds(6 * par, 2)], swap_with, h)

    def start(*copies):
        for c in copies:
            c.start()

    def arrived(*copies):
        for c in copies:
            c.wait_recv()

    start(*near_edge, desc_up, desc_dn, corner)
    loads = [
        pltpu.make_async_copy(data, x.at[:, pl.ds(4, 4)], load.at[0]),
        pltpu.make_async_copy(desc, dd.at[pl.ds(4, 4)], load.at[1]),
        pltpu.make_async_copy(compat_in, compat, load.at[2]),
        pltpu.make_async_copy(off_in, off, load.at[3]),
    ]
    for c in loads:
        c.start()
    for c in loads:
        c.wait()

    def loop(count_, body):
        lax.fori_loop(0, count_, lambda i, c: (body(i), c)[1], 0)

    def soft_to(src, dst, flag):
        for j in range(4):
            cols = pl.ds(128 * j, 128)
            w = jnp.exp(-src[:, cols].astype(F32))
            inv = flag / jnp.sum(w, axis=0, keepdims=True)
            dst[:, cols] = (w * inv).astype(BF)

    def flag_of(e):
        return jnp.where(e < 4, below, jnp.where(e > 7, above, 1.0))

    def transpose(e):
        dt[e] = jnp.transpose(dd[e].astype(F32)).astype(BF)

    def project(e, src, dst):
        dst[...] = jnp.dot(dt[e], src[...], preferred_element_type=F32).astype(BF)

    lane512 = lax.broadcasted_iota(jnp.int32, (LAB, COLS), 1)

    def gather(near, far, planes, centre, s_buf):
        half = jnp.asarray(0.5, BF)
        cc = centre[...]
        lf = jnp.where(lane512 > 0, pltpu.roll(cc, 1, 1), jnp.zeros_like(cc))
        rt = jnp.where(lane512 < COLS - 1, pltpu.roll(cc, COLS - 1, 1), jnp.zeros_like(cc))
        lr = lf + rt
        for j in range(COLS // 256):
            cols = pl.ds(256 * j, 256)
            z = (near[0][:, cols] + near[1][:, cols]) + half * (far[0][:, cols] + far[1][:, cols])
            p = planes[0][:, cols]
            for q in planes[1:]:
                p = p + q[:, cols]
            s_buf[:, cols] = lr[:, 256 * j : 256 * j + 256] + p + z

    def gather_p(a, b, c, g, ps_buf):
        ps_buf[...] = (a[...] + b[...]) + (c[...] + g[...])

    def energy_of(e, dref, cols, s_buf, ps_buf):
        v = dref[:, cols].astype(F32)
        v = v + jnp.dot(compat[...], s_buf[:, cols], preferred_element_type=F32)
        return v + jnp.dot(dd[e], ps_buf[:, cols], preferred_element_type=F32)

    def norm(v, flag):
        w = jnp.exp(-v)
        inv = flag / jnp.sum(w, axis=0, keepdims=True)
        return (w * inv).astype(BF)

    def pairs(count_, *phases):
        def body(i):
            for phase in phases:
                for u in range(2):
                    phase(2 * i + u, u)
        loop(count_ // 2, body)

    def sweep1(q, at, count_):
        r = row(q)

        def collect(i, u):
            e = at(i)
            planes = []
            if q > 0:
                planes.append(m0.at[row(q - 1), e])
            planes.append(m0.at[row(q + 1), e] if q < 3 else m0r.at[e - 2])
            gather((m0.at[r, e - 1], m0.at[r, e + 1]), (m0.at[r, e - 2], m0.at[r, e + 2]), planes, m0.at[r, e], s_bufs[u])
            gather_p(p0.at[r, e - 1], p0.at[r, e + 1], p0.at[r, e - 2], p0.at[r, e + 2], ps_bufs[u])

        def settle(i, u):
            e = at(i)
            for j in range(2):
                cols = pl.ds(256 * j, 256)
                m1.at[r, e - 2][:, cols] = norm(energy_of(e, x.at[r, e], cols, s_bufs[u], ps_bufs[u]), flag_of(e))

        def forward(i, u):
            e = at(i)
            project(e, m1.at[r, e - 2], p1.at[r, e - 2])

        pairs(count_, collect, settle, forward)

    def sweep1_rim():
        def collect(i, u):
            e, t = 4 + i, 2 + i
            gather((m0r.at[t - 1], m0r.at[t + 1]), (m0r.at[t - 2], m0r.at[t + 2]), [m0.at[row(3), e], m0r.at[8 + i]], m0r.at[t], s_bufs[u])
            gather_p(p0r.at[t - 1], p0r.at[t + 1], p0r.at[t - 2], p0r.at[t + 2], ps_bufs[u])

        def settle(i, u):
            for j in range(2):
                cols = pl.ds(256 * j, 256)
                m0r.at[8 + i][:, cols] = norm(energy_of(4 + i, xr.at[h, 2 + i], cols, s_bufs[u], ps_bufs[u]), 1.0)

        pairs(4, collect, settle)

    def copy_out(r, k, u):
        return pltpu.make_async_copy(stage.at[u], out.at[k, :, r, :], store.at[u])

    def sweep2(q, first_use):
        r = row(q)

        def collect(k, u):
            t = 2 + k
            planes = []
            if q > 0:
                planes.append(m1.at[row(q - 1), t])
            planes.append(m1.at[row(q + 1), t] if q < 3 else m0r.at[8 + k])
            gather((m1.at[r, t - 1], m1.at[r, t + 1]), (m1.at[r, t - 2], m1.at[r, t + 2]), planes, m1.at[r, t], s_bufs[u])
            gather_p(p1.at[r, t - 1], p1.at[r, t + 1], p1.at[r, t - 2], p1.at[r, t + 2], ps_bufs[u])

        def settle(k, u):
            if first_use:
                @pl.when(k >= 2)
                def _():
                    copy_out(r, k, u).wait()
            else:
                copy_out(r, k, u).wait()
            for j in range(2):
                cols = pl.ds(256 * j, 256)
                v = energy_of(4 + k, x.at[r, 4 + k], cols, s_bufs[u], ps_bufs[u])
                stage.at[u][:, cols] = v
                disp.at[k, r][:, cols] = jnp.dot(off[...], norm(v, 1.0), preferred_element_type=F32)
            copy_out(r, k, u).start()

        pairs(4, collect, settle)

    def wing(i):
        return 2 + i + 4 * lax.div(i, 2)

    def tip(i):
        return i + 8 * lax.div(i, 2)

    def own(i):
        return 4 + i

    def first(count_, at):
        def soft(i, u):
            r, e = at(i)
            soft_to(x.at[r, e], m0.at[r, e], flag_of(e))

        def proj(i, u):
            r, e = at(i)
            project(e, m0.at[r, e], p0.at[r, e])

        pairs(count_, soft, proj)

    loop(4, lambda i: transpose(4 + i))
    first(16, lambda i: (lax.div(i, 4), 4 + lax.rem(i, 4)))

    arrived(*near_edge)
    start(*far_edge, relay_near)
    arrived(desc_up, desc_dn)
    loop(8, lambda i: transpose(i + 4 * lax.div(i, 4)))
    first(8, lambda i: (row(2 + lax.div(i, 4)), wing(lax.rem(i, 4))))
    sweep1(2, own, 4)
    arrived(*far_edge)
    start(*near_rest, relay_far)
    first(8, lambda i: (row(2 + lax.div(i, 4)), tip(lax.rem(i, 4))))
    arrived(corner, relay_near, relay_far)
    swap.start()
    arrived(swap)

    arrived(*near_rest)
    start(*far_one, *far_zero)
    first(8, lambda i: (row(lax.div(i, 4)), wing(lax.rem(i, 4))))

    def rim_soft(t, u):
        soft_to(xr.at[h, t], m0r.at[t], flag_of(t + 2))

    def rim_proj(t, u):
        project(t + 2, m0r.at[t], p0r.at[t])

    pairs(8, rim_soft, rim_proj)
    pairs(4, lambda i, u: soft_to(xr.at[other, i + 2], m0r.at[8 + i], 1.0))
    sweep1_rim()
    sweep1(3, lambda i: 2 + i, 8)
    sweep1(2, wing, 4)
    sweep1(1, own, 4)
    sweep1(0, own, 4)
    sweep2(3, True)
    sweep2(2, False)

    for q, copies in ((1, far_one), (0, far_zero)):
        arrived(*copies)
        first(4, lambda i: (row(q), tip(i)))
        sweep1(q, wing, 4)
        sweep2(q, False)
    for u in range(2):
        copy_out(row(0), u, u).wait()
    for c in (*near_edge, *far_edge, *near_rest, *far_one, *far_zero, desc_up, desc_dn, corner, relay_near, relay_far, swap):
        c.wait_send()


def on_device(n, unary_cost, descriptors, valid_rows, offsets):
    data = jnp.transpose(unary_cost, (1, 0, 2, 3)) * valid_rows.astype(BF).T[:, :, None, None]
    co = offsets.astype(F32)
    spread = jnp.abs(co[:, None, 0] - co[None, :, 0]) + jnp.abs(co[:, None, 1] - co[None, :, 1])
    compat = (0.125 * jnp.minimum(spread, 6.0)).astype(BF)
    off8 = jnp.concatenate([offsets.T, jnp.zeros((6, LAB), offsets.dtype)], axis=0).astype(BF)
    hbm = pl.BlockSpec(memory_space=pl.ANY)
    e, disp = pl.pallas_call(
        functools.partial(kernel, n),
        in_specs=[hbm] * 4,
        out_specs=[hbm, pl.BlockSpec(memory_space=pltpu.VMEM)],
        out_shape=[jax.ShapeDtypeStruct((4, LAB, 4, COLS), F32), jax.ShapeDtypeStruct((4, 4, 8, COLS), F32)],
        scratch_shapes=[
            pltpu.VMEM((4, 12, LAB, COLS), BF),
            pltpu.VMEM((2, 8, LAB, COLS), BF),
            pltpu.VMEM((4, 12, LAB, COLS), BF),
            pltpu.VMEM((12, LAB, COLS), BF),
            pltpu.VMEM((4, 12, FEAT, COLS), BF),
            pltpu.VMEM((8, FEAT, COLS), BF),
            pltpu.VMEM((4, 8, FEAT, COLS), BF),
            pltpu.VMEM((4, 8, LAB, COLS), BF),
            pltpu.VMEM((12, LAB, FEAT), BF),
            pltpu.VMEM((12, FEAT, LAB), BF),
            pltpu.VMEM((LAB, LAB), BF),
            pltpu.VMEM((8, LAB), BF),
            pltpu.VMEM((LAB, COLS), BF),
            pltpu.VMEM((LAB, COLS), BF),
            pltpu.VMEM((FEAT, COLS), BF),
            pltpu.VMEM((FEAT, COLS), BF),
            pltpu.VMEM((2, LAB, COLS), F32),
            pltpu.SemaphoreType.DMA((16,)),
            pltpu.SemaphoreType.DMA((16,)),
            pltpu.SemaphoreType.DMA((4,)),
            pltpu.SemaphoreType.DMA((2,)),
        ],
        compiler_params=pltpu.CompilerParams(collective_id=0, has_side_effects=True, vmem_limit_bytes=67043328),
        name="mega",
    )(data, descriptors, compat, off8)
    return jnp.transpose(e, (0, 2, 1, 3)), jnp.transpose(disp[:, :, 0:2], (2, 0, 1, 3))


def solution(mesh):
    in_specs = (P("gz", "rows", None, None), P("gz", None, None), P("gz", "rows"), P())
    out_specs = (P("gz", "rows", None, None), P(None, "gz", "rows", None))
    return jax.shard_map(functools.partial(on_device, mesh.shape["gz"]), mesh=mesh, in_specs=in_specs, out_specs=out_specs, check_vma=False)
```

```python
import functools

import jax
import jax.numpy as jnp
from jax import lax
from jax.experimental import pallas as pl
from jax.experimental.pallas import tpu as pltpu
from jax.sharding import PartitionSpec as P

BF = jnp.bfloat16
F32 = jnp.float32
MESH = pl.DeviceIdType.MESH
LAB = 225
FEAT = 256
COLS = 512


def kernel(n, data, desc, off_in, out, disp, x, xr, m0, m0r, p0, p0r, p1, m1, dd, dt, compat, off, s0, s1, ps0, ps1, stage, send, recv, load, store):
    d = lax.axis_index("gz")
    h = lax.axis_index("rows")
    par = lax.rem(d, 2)
    prev = lax.rem(d + n - 1, n)
    nxt = lax.rem(d + 1, n)
    other = 1 - h
    relay_to = lax.rem(d + n - 1 + 2 * par, n)
    swap_with = d + 1 - 2 * par
    r0 = 2 - 2 * h
    s_bufs = (s0, s1)
    ps_bufs = (ps0, ps1)
    r_edge = 3 - 3 * h
    below = jnp.where(d > 0, 1.0, 0.0).astype(F32)
    above = jnp.where(d < n - 1, 1.0, 0.0).astype(F32)

    def row(q):
        return q + h * (3 - 2 * q)

    barrier = pltpu.get_barrier_semaphore()
    for g in (prev, nxt):
        for k in (h, other):
            pl.semaphore_signal(barrier, inc=1, device_id=(g, k), device_id_type=MESH)
    pl.semaphore_wait(barrier, 4)

    count = [0]

    def remote(src, dst, g, k):
        i = count[0]
        count[0] += 1
        return pltpu.make_async_remote_copy(src_ref=src, dst_ref=dst, send_sem=send.at[i], recv_sem=recv.at[i], device_id=(g, k), device_id_type=MESH)

    def blocks(rows, up_s, up_e, dn_s, dn_e):
        return (
            remote(data.at[rows, pl.ds(up_s, 2)], x.at[rows, pl.ds(up_e, 2)], nxt, h),
            remote(data.at[rows, pl.ds(dn_s, 2)], x.at[rows, pl.ds(dn_e, 2)], prev, h),
        )

    edge_rows = pl.ds(r0, 2)
    near_edge = blocks(edge_rows, 2, 2, 0, 8)
    far_edge = blocks(edge_rows, 0, 0, 2, 10)
    near_one = blocks(pl.ds(row(1), 1), 2, 2, 0, 8)
    near_zero = blocks(pl.ds(row(0), 1), 2, 2, 0, 8)
    far_one = blocks(pl.ds(row(1), 1), 0, 0, 2, 10)
    far_zero = blocks(pl.ds(row(0), 1), 0, 0, 2, 10)
    desc_up = remote(desc, dd.at[pl.ds(0, 4)], nxt, jnp.where(par == 0, h, other))
    desc_dn = remote(desc, dd.at[pl.ds(8, 4)], prev, jnp.where(par == 0, other, h))
    corner = remote(data.at[r_edge, pl.ds(2 * par, 2)], xr.at[other, pl.ds(6 - 6 * par, 2)], relay_to, other)
    relay_near = remote(x.at[edge_rows, pl.ds(2 + 6 * par, 2)], xr.at[:, pl.ds(4 - 2 * par, 2)], relay_to, other)
    relay_far = remote(x.at[r_edge, pl.ds(10 * par, 2)], xr.at[other, pl.ds(2 + 2 * par, 2)], relay_to, other)
    relay_last = remote(x.at[row(2), pl.ds(10 * par, 2)], xr.at[h, pl.ds(2 + 2 * par, 2)], relay_to, other)
    swap = remote(xr.at[h, pl.ds(4 - 2 * par, 2)], xr.at[h, pl.ds(6 * par, 2)], swap_with, h)

    def start(*copies):
        for c in copies:
            c.start()

    def arrived(*copies):
        for c in copies:
            c.wait_recv()

    start(*near_edge, desc_up, desc_dn, corner)
    loads = [
        pltpu.make_async_copy(data, x.at[:, pl.ds(4, 4)], load.at[0]),
        pltpu.make_async_copy(desc, dd.at[pl.ds(4, 4)], load.at[1]),
    ]
    for c in loads:
        c.start()
    for c in loads:
        c.wait()

    def loop(count_, body):
        lax.fori_loop(0, count_, lambda i, c: (body(i), c)[1], 0)

    def soft_to(src, dst, flag):
        for j in range(4):
            cols = pl.ds(128 * j, 128)
            w = jnp.exp(-src[:, cols].astype(F32))
            inv = flag / jnp.sum(w, axis=0, keepdims=True)
            dst[:, cols] = (w * inv).astype(BF)

    def flag_of(e):
        return jnp.where(e < 4, below, jnp.where(e > 7, above, 1.0))

    def transpose(e):
        dt[e] = jnp.transpose(dd[e].astype(F32)).astype(BF)

    def project(e, src, dst):
        dst[...] = jnp.dot(dt[e], src[...], preferred_element_type=F32).astype(BF)

    lane512 = lax.broadcasted_iota(jnp.int32, (LAB, COLS), 1)

    def gather(near, far, planes, centre, s_buf):
        half = jnp.asarray(0.5, BF)
        cc = centre[...]
        lf = jnp.where(lane512 > 0, pltpu.roll(cc, 1, 1), jnp.zeros_like(cc))
        rt = jnp.where(lane512 < COLS - 1, pltpu.roll(cc, COLS - 1, 1), jnp.zeros_like(cc))
        lr = lf + rt
        for j in range(COLS // 256):
            cols = pl.ds(256 * j, 256)
            z = (near[0][:, cols] + near[1][:, cols]) + half * (far[0][:, cols] + far[1][:, cols])
            p = planes[0][:, cols]
            for q in planes[1:]:
                p = p + q[:, cols]
            s_buf[:, cols] = lr[:, 256 * j : 256 * j + 256] + p + z

    def gather_p(a, b, c, g, ps_buf):
        ps_buf[...] = (a[...] + b[...]) + (c[...] + g[...])

    def energy_of(e, dref, cols, s_buf, ps_buf):
        v = dref[:, cols].astype(F32)
        v = v + jnp.dot(compat[...], s_buf[:, cols], preferred_element_type=F32)
        return v + jnp.dot(dd[e], ps_buf[:, cols], preferred_element_type=F32)

    def norm(v, flag):
        w = jnp.exp(-v)
        inv = flag / jnp.sum(w, axis=0, keepdims=True)
        return (w * inv).astype(BF)

    def pairs(count_, *phases):
        def body(i):
            for phase in phases:
                for u in range(2):
                    phase(2 * i + u, u)
        loop(count_ // 2, body)

    def sweep1(q, at, count_):
        r = row(q)

        def collect(i, u):
            e = at(i)
            planes = []
            if q > 0:
                planes.append(m0.at[row(q - 1), e])
            planes.append(m0.at[row(q + 1), e] if q < 3 else m0r.at[e - 2])
            gather((m0.at[r, e - 1], m0.at[r, e + 1]), (m0.at[r, e - 2], m0.at[r, e + 2]), planes, m0.at[r, e], s_bufs[u])
            gather_p(p0.at[r, e - 1], p0.at[r, e + 1], p0.at[r, e - 2], p0.at[r, e + 2], ps_bufs[u])

        def settle(i, u):
            e = at(i)
            for j in range(2):
                cols = pl.ds(256 * j, 256)
                m1.at[r, e - 2][:, cols] = norm(energy_of(e, x.at[r, e], cols, s_bufs[u], ps_bufs[u]), flag_of(e))

        def forward(i, u):
            e = at(i)
            project(e, m1.at[r, e - 2], p1.at[r, e - 2])

        pairs(count_, collect, settle, forward)

    def sweep1_rim():
        def collect(i, u):
            e, t = 4 + i, 2 + i
            gather((m0r.at[t - 1], m0r.at[t + 1]), (m0r.at[t - 2], m0r.at[t + 2]), [m0.at[row(3), e], m0r.at[8 + i]], m0r.at[t], s_bufs[u])
            gather_p(p0r.at[t - 1], p0r.at[t + 1], p0r.at[t - 2], p0r.at[t + 2], ps_bufs[u])

        def settle(i, u):
            for j in range(2):
                cols = pl.ds(256 * j, 256)
                m0r.at[8 + i][:, cols] = norm(energy_of(4 + i, xr.at[h, 2 + i], cols, s_bufs[u], ps_bufs[u]), 1.0)

        pairs(4, collect, settle)

    def copy_out(r, k, u):
        return pltpu.make_async_copy(stage.at[u], out.at[k, :, r, :], store.at[u])

    def sweep2(q, first_use):
        r = row(q)

        def collect(k, u):
            t = 2 + k
            planes = []
            if q > 0:
                planes.append(m1.at[row(q - 1), t])
            planes.append(m1.at[row(q + 1), t] if q < 3 else m0r.at[8 + k])
            gather((m1.at[r, t - 1], m1.at[r, t + 1]), (m1.at[r, t - 2], m1.at[r, t + 2]), planes, m1.at[r, t], s_bufs[u])
            gather_p(p1.at[r, t - 1], p1.at[r, t + 1], p1.at[r, t - 2], p1.at[r, t + 2], ps_bufs[u])

        def settle(k, u):
            if first_use:
                @pl.when(k >= 2)
                def _():
                    copy_out(r, k, u).wait()
            else:
                copy_out(r, k, u).wait()
            for j in range(2):
                cols = pl.ds(256 * j, 256)
                v = energy_of(4 + k, x.at[r, 4 + k], cols, s_bufs[u], ps_bufs[u])
                stage.at[u][:, cols] = v
                disp.at[k, r][:, cols] = jnp.dot(off[...].astype(BF), norm(v, 1.0), preferred_element_type=F32)
            copy_out(r, k, u).start()

        pairs(4, collect, settle)

    def wing(i):
        return 2 + i + 4 * lax.div(i, 2)

    def tip(i):
        return i + 8 * lax.div(i, 2)

    def own(i):
        return 4 + i

    def first(count_, at):
        def soft(i, u):
            r, e = at(i)
            soft_to(x.at[r, e], m0.at[r, e], flag_of(e))

        def proj(i, u):
            r, e = at(i)
            project(e, m0.at[r, e], p0.at[r, e])

        pairs(count_, soft, proj)

    off[...] = jnp.concatenate([off_in[...].astype(F32), jnp.zeros((6, LAB), F32)], axis=0)
    turned = jnp.transpose(off[...])
    spread = jnp.abs(turned[:, 0:1] - off[0:1, :]) + jnp.abs(turned[:, 1:2] - off[1:2, :])
    compat[...] = (0.125 * jnp.minimum(spread, 6.0)).astype(BF)

    loop(4, lambda i: transpose(4 + i))
    first(16, lambda i: (lax.div(i, 4), 4 + lax.rem(i, 4)))

    half = 4 * par

    def rim(slot):
        def rim_soft(i, u):
            soft_to(xr.at[h, slot + i], m0r.at[slot + i], flag_of(slot + i + 2))

        def rim_proj(i, u):
            project(slot + i + 2, m0r.at[slot + i], p0r.at[slot + i])

        pairs(4, rim_soft, rim_proj)
        sweep1(3, lambda i: 2 + slot + i, 4)

    start(*far_edge)
    arrived(*near_edge)
    start(relay_near)
    arrived(desc_up, desc_dn)
    loop(8, lambda i: transpose(i + 4 * lax.div(i, 4)))
    first(8, lambda i: (row(2 + lax.div(i, 4)), wing(lax.rem(i, 4))))
    sweep1(2, own, 4)
    start(*near_one)
    arrived(*far_edge)
    start(relay_far, *near_zero)
    first(8, lambda i: (row(2 + lax.div(i, 4)), tip(lax.rem(i, 4))))

    arrived(*near_one)
    start(*far_one)
    first(4, lambda i: (row(1), wing(i)))
    sweep1(2, wing, 4)
    arrived(relay_far)
    start(swap, relay_last)
    sweep1(1, own, 4)
    arrived(corner, relay_near)
    rim(half)
    arrived(*near_zero)
    start(*far_zero)
    first(4, lambda i: (row(0), wing(i)))
    sweep1(0, own, 4)
    arrived(swap, relay_last)
    rim(4 - half)
    pairs(4, lambda i, u: soft_to(xr.at[other, i + 2], m0r.at[8 + i], 1.0))
    sweep1_rim()
    sweep2(3, True)
    sweep2(2, False)

    for q, copies in ((1, far_one), (0, far_zero)):
        arrived(*copies)
        first(4, lambda i: (row(q), tip(i)))
        sweep1(q, wing, 4)
        sweep2(q, False)
    for u in range(2):
        copy_out(row(0), u, u).wait()
    for c in (*near_edge, *far_edge, *near_one, *near_zero, *far_one, *far_zero, desc_up, desc_dn, corner, relay_near, relay_far, relay_last, swap):
        c.wait_send()


def on_device(n, unary_cost, descriptors, valid_rows, offsets):
    data = jnp.transpose(unary_cost, (1, 0, 2, 3)) * valid_rows.astype(BF).T[:, :, None, None]
    hbm = pl.BlockSpec(memory_space=pl.ANY)
    e, disp = pl.pallas_call(
        functools.partial(kernel, n),
        in_specs=[hbm, hbm, pl.BlockSpec(memory_space=pltpu.VMEM)],
        out_specs=[hbm, pl.BlockSpec(memory_space=pltpu.VMEM)],
        out_shape=[jax.ShapeDtypeStruct((4, LAB, 4, COLS), F32), jax.ShapeDtypeStruct((4, 4, 8, COLS), F32)],
        scratch_shapes=[
            pltpu.VMEM((4, 12, LAB, COLS), BF),
            pltpu.VMEM((2, 8, LAB, COLS), BF),
            pltpu.VMEM((4, 12, LAB, COLS), BF),
            pltpu.VMEM((12, LAB, COLS), BF),
            pltpu.VMEM((4, 12, FEAT, COLS), BF),
            pltpu.VMEM((8, FEAT, COLS), BF),
            pltpu.VMEM((4, 8, FEAT, COLS), BF),
            pltpu.VMEM((4, 8, LAB, COLS), BF),
            pltpu.VMEM((12, LAB, FEAT), BF),
            pltpu.VMEM((12, FEAT, LAB), BF),
            pltpu.VMEM((LAB, LAB), BF),
            pltpu.VMEM((8, LAB), F32),
            pltpu.VMEM((LAB, COLS), BF),
            pltpu.VMEM((LAB, COLS), BF),
            pltpu.VMEM((FEAT, COLS), BF),
            pltpu.VMEM((FEAT, COLS), BF),
            pltpu.VMEM((2, LAB, COLS), F32),
            pltpu.SemaphoreType.DMA((19,)),
            pltpu.SemaphoreType.DMA((19,)),
            pltpu.SemaphoreType.DMA((2,)),
            pltpu.SemaphoreType.DMA((2,)),
        ],
        compiler_params=pltpu.CompilerParams(collective_id=0, has_side_effects=True, vmem_limit_bytes=67043328),
        name="mega",
    )(data, descriptors, offsets.T)
    return jnp.transpose(e, (0, 2, 1, 3)), jnp.transpose(disp[:, :, 0:2], (2, 0, 1, 3))


def solution(mesh):
    in_specs = (P("gz", "rows", None, None), P("gz", None, None), P("gz", "rows"), P())
    out_specs = (P("gz", "rows", None, None), P(None, "gz", "rows", None))
    return jax.shard_map(functools.partial(on_device, mesh.shape["gz"]), mesh=mesh, in_specs=in_specs, out_specs=out_specs, check_vma=False)
```

```python
import functools

import jax
import jax.numpy as jnp
from jax import lax
from jax.experimental import pallas as pl
from jax.experimental.pallas import tpu as pltpu
from jax.sharding import PartitionSpec as P

BF = jnp.bfloat16
F32 = jnp.float32
MESH = pl.DeviceIdType.MESH
LAB = 225
FEAT = 256
COLS = 512


def kernel(n, data, desc, off_in, out, disp, x, xr, m0, m0r, p0, p0r, p1, m1, dd, dt, compat, off, s0, s1, ps0, ps1, stage, send, recv, load, store):
    d = lax.axis_index("gz")
    h = lax.axis_index("rows")
    par = lax.rem(d, 2)
    prev = lax.rem(d + n - 1, n)
    nxt = lax.rem(d + 1, n)
    other = 1 - h
    relay_to = lax.rem(d + n - 1 + 2 * par, n)
    swap_with = d + 1 - 2 * par
    r0 = 2 - 2 * h
    s_bufs = (s0, s1)
    ps_bufs = (ps0, ps1)
    r_edge = 3 - 3 * h
    below = jnp.where(d > 0, 1.0, 0.0).astype(F32)
    above = jnp.where(d < n - 1, 1.0, 0.0).astype(F32)

    def row(q):
        return q + h * (3 - 2 * q)

    barrier = pltpu.get_barrier_semaphore()
    for g in (prev, nxt):
        for k in (h, other):
            pl.semaphore_signal(barrier, inc=1, device_id=(g, k), device_id_type=MESH)
    pl.semaphore_wait(barrier, 4)

    count = [0]

    def remote(src, dst, g, k):
        i = count[0]
        count[0] += 1
        return pltpu.make_async_remote_copy(src_ref=src, dst_ref=dst, send_sem=send.at[i], recv_sem=recv.at[i], device_id=(g, k), device_id_type=MESH)

    def blocks(rows, up_s, up_e, dn_s, dn_e):
        return (
            remote(data.at[rows, pl.ds(up_s, 2)], x.at[rows, pl.ds(up_e, 2)], nxt, h),
            remote(data.at[rows, pl.ds(dn_s, 2)], x.at[rows, pl.ds(dn_e, 2)], prev, h),
        )

    edge_rows = pl.ds(r0, 2)
    near_edge = blocks(edge_rows, 2, 2, 0, 8)
    far_edge = blocks(edge_rows, 0, 0, 2, 10)
    near_one = blocks(pl.ds(row(1), 1), 2, 2, 0, 8)
    near_zero = blocks(pl.ds(row(0), 1), 2, 2, 0, 8)
    far_one = blocks(pl.ds(row(1), 1), 0, 0, 2, 10)
    far_zero = blocks(pl.ds(row(0), 1), 0, 0, 2, 10)
    desc_up = remote(desc, dd.at[pl.ds(0, 4)], nxt, jnp.where(par == 0, h, other))
    desc_dn = remote(desc, dd.at[pl.ds(8, 4)], prev, jnp.where(par == 0, other, h))
    corner = remote(data.at[r_edge, pl.ds(2 * par, 2)], xr.at[other, pl.ds(6 - 6 * par, 2)], relay_to, other)
    relay_near = remote(x.at[edge_rows, pl.ds(2 + 6 * par, 2)], xr.at[:, pl.ds(4 - 2 * par, 2)], relay_to, other)
    relay_far = remote(x.at[r_edge, pl.ds(10 * par, 2)], xr.at[other, pl.ds(2 + 2 * par, 2)], relay_to, other)
    relay_last = remote(x.at[row(2), pl.ds(10 * par, 2)], xr.at[h, pl.ds(2 + 2 * par, 2)], relay_to, other)
    swap = remote(xr.at[h, pl.ds(4 - 2 * par, 2)], xr.at[h, pl.ds(6 * par, 2)], swap_with, h)

    def start(*copies):
        for c in copies:
            c.start()

    def arrived(*copies):
        for c in copies:
            c.wait_recv()

    start(*near_edge, desc_up, desc_dn, corner)
    loads = [
        pltpu.make_async_copy(data, x.at[:, pl.ds(4, 4)], load.at[0]),
        pltpu.make_async_copy(desc, dd.at[pl.ds(4, 4)], load.at[1]),
    ]
    for c in loads:
        c.start()
    for c in loads:
        c.wait()

    def loop(count_, body):
        lax.fori_loop(0, count_, lambda i, c: (body(i), c)[1], 0)

    def soft_to(src, dst, flag):
        for j in range(4):
            cols = pl.ds(128 * j, 128)
            w = jnp.exp(-src[:, cols].astype(F32))
            inv = flag / jnp.sum(w, axis=0, keepdims=True)
            dst[:, cols] = (w * inv).astype(BF)

    def flag_of(e):
        return jnp.where(e < 4, below, jnp.where(e > 7, above, 1.0))

    def transpose(e):
        dt[e] = jnp.transpose(dd[e].astype(F32)).astype(BF)

    def project(e, src, dst):
        dst[...] = jnp.dot(dt[e], src[...], preferred_element_type=F32).astype(BF)

    lane512 = lax.broadcasted_iota(jnp.int32, (LAB, COLS), 1)

    def gather(near, far, planes, centre, s_buf):
        half = jnp.asarray(0.5, BF)
        cc = centre[...]
        lf = jnp.where(lane512 > 0, pltpu.roll(cc, 1, 1), jnp.zeros_like(cc))
        rt = jnp.where(lane512 < COLS - 1, pltpu.roll(cc, COLS - 1, 1), jnp.zeros_like(cc))
        lr = lf + rt
        for j in range(COLS // 256):
            cols = pl.ds(256 * j, 256)
            z = (near[0][:, cols] + near[1][:, cols]) + half * (far[0][:, cols] + far[1][:, cols])
            p = planes[0][:, cols]
            for q in planes[1:]:
                p = p + q[:, cols]
            s_buf[:, cols] = lr[:, 256 * j : 256 * j + 256] + p + z

    def gather_p(a, b, c, g, ps_buf):
        ps_buf[...] = (a[...] + b[...]) + (c[...] + g[...])

    def energy_of(e, dref, cols, s_buf, ps_buf):
        v = dref[:, cols].astype(F32)
        v = v + jnp.dot(compat[...], s_buf[:, cols], preferred_element_type=F32)
        return v + jnp.dot(dd[e], ps_buf[:, cols], preferred_element_type=F32)

    def norm(v, flag):
        w = jnp.exp(-v)
        inv = flag / jnp.sum(w, axis=0, keepdims=True)
        return (w * inv).astype(BF)

    def pairs(count_, *phases):
        def body(i):
            for phase in phases:
                for u in range(2):
                    phase(2 * i + u, u)
        loop(count_ // 2, body)

    def sweep1(q, at, count_):
        r = row(q)

        def collect(i, u):
            e = at(i)
            planes = []
            if q > 0:
                planes.append(m0.at[row(q - 1), e])
            planes.append(m0.at[row(q + 1), e] if q < 3 else m0r.at[e - 2])
            gather((m0.at[r, e - 1], m0.at[r, e + 1]), (m0.at[r, e - 2], m0.at[r, e + 2]), planes, m0.at[r, e], s_bufs[u])
            gather_p(p0.at[r, e - 1], p0.at[r, e + 1], p0.at[r, e - 2], p0.at[r, e + 2], ps_bufs[u])

        def settle(i, u):
            e = at(i)
            for j in range(2):
                cols = pl.ds(256 * j, 256)
                m1.at[r, e - 2][:, cols] = norm(energy_of(e, x.at[r, e], cols, s_bufs[u], ps_bufs[u]), flag_of(e))

        def forward(i, u):
            e = at(i)
            project(e, m1.at[r, e - 2], p1.at[r, e - 2])

        pairs(count_, collect, settle, forward)

    def sweep1_rim():
        def collect(i, u):
            e, t = 4 + i, 2 + i
            gather((m0r.at[t - 1], m0r.at[t + 1]), (m0r.at[t - 2], m0r.at[t + 2]), [m0.at[row(3), e], m0r.at[8 + i]], m0r.at[t], s_bufs[u])
            gather_p(p0r.at[t - 1], p0r.at[t + 1], p0r.at[t - 2], p0r.at[t + 2], ps_bufs[u])

        def settle(i, u):
            for j in range(2):
                cols = pl.ds(256 * j, 256)
                m0r.at[8 + i][:, cols] = norm(energy_of(4 + i, xr.at[h, 2 + i], cols, s_bufs[u], ps_bufs[u]), 1.0)

        pairs(4, collect, settle)

    def copy_out(r, k, u):
        return pltpu.make_async_copy(stage.at[u], out.at[k, :, r, :], store.at[u])

    def sweep2(q, first_use):
        r = row(q)

        def collect(k, u):
            t = 2 + k
            planes = []
            if q > 0:
                planes.append(m1.at[row(q - 1), t])
            planes.append(m1.at[row(q + 1), t] if q < 3 else m0r.at[8 + k])
            gather((m1.at[r, t - 1], m1.at[r, t + 1]), (m1.at[r, t - 2], m1.at[r, t + 2]), planes, m1.at[r, t], s_bufs[u])
            gather_p(p1.at[r, t - 1], p1.at[r, t + 1], p1.at[r, t - 2], p1.at[r, t + 2], ps_bufs[u])

        def settle(k, u):
            if first_use:
                @pl.when(k >= 2)
                def _():
                    copy_out(r, k, u).wait()
            else:
                copy_out(r, k, u).wait()
            for j in range(2):
                cols = pl.ds(256 * j, 256)
                v = energy_of(4 + k, x.at[r, 4 + k], cols, s_bufs[u], ps_bufs[u])
                stage.at[u][:, cols] = v
                mean = jnp.dot(off[...].astype(BF), norm(v, 1.0), preferred_element_type=F32)
                for axis in range(2):
                    disp[axis, k, pl.ds(r, 1), cols] = mean[axis : axis + 1]
            copy_out(r, k, u).start()

        pairs(4, collect, settle)

    def wing(i):
        return 2 + i + 4 * lax.div(i, 2)

    def tip(i):
        return i + 8 * lax.div(i, 2)

    def own(i):
        return 4 + i

    def first(count_, at):
        def soft(i, u):
            r, e = at(i)
            soft_to(x.at[r, e], m0.at[r, e], flag_of(e))

        def proj(i, u):
            r, e = at(i)
            project(e, m0.at[r, e], p0.at[r, e])

        pairs(count_, soft, proj)

    off[...] = jnp.concatenate([off_in[...].astype(F32), jnp.zeros((6, LAB), F32)], axis=0)
    turned = jnp.transpose(off[...])
    spread = jnp.abs(turned[:, 0:1] - off[0:1, :]) + jnp.abs(turned[:, 1:2] - off[1:2, :])
    compat[...] = (0.125 * jnp.minimum(spread, 6.0)).astype(BF)

    loop(4, lambda i: transpose(4 + i))
    first(16, lambda i: (lax.div(i, 4), 4 + lax.rem(i, 4)))

    half = 4 * par

    def rim(slot):
        def rim_soft(i, u):
            soft_to(xr.at[h, slot + i], m0r.at[slot + i], flag_of(slot + i + 2))

        def rim_proj(i, u):
            project(slot + i + 2, m0r.at[slot + i], p0r.at[slot + i])

        pairs(4, rim_soft, rim_proj)
        sweep1(3, lambda i: 2 + slot + i, 4)

    start(*far_edge)
    arrived(*near_edge)
    start(relay_near)
    arrived(desc_up, desc_dn)
    loop(8, lambda i: transpose(i + 4 * lax.div(i, 4)))
    first(8, lambda i: (row(2 + lax.div(i, 4)), wing(lax.rem(i, 4))))
    sweep1(2, own, 4)
    start(*near_one)
    arrived(*far_edge)
    start(relay_far, *near_zero)
    first(8, lambda i: (row(2 + lax.div(i, 4)), tip(lax.rem(i, 4))))

    arrived(*near_one)
    start(*far_one)
    first(4, lambda i: (row(1), wing(i)))
    sweep1(2, wing, 4)
    arrived(relay_far)
    start(swap, relay_last)
    sweep1(1, own, 4)
    arrived(corner, relay_near)
    rim(half)
    arrived(*near_zero)
    start(*far_zero)
    first(4, lambda i: (row(0), wing(i)))
    sweep1(0, own, 4)
    arrived(swap, relay_last)
    rim(4 - half)
    pairs(4, lambda i, u: soft_to(xr.at[other, i + 2], m0r.at[8 + i], 1.0))
    sweep1_rim()
    sweep2(3, True)
    sweep2(2, False)

    for q, copies in ((1, far_one), (0, far_zero)):
        arrived(*copies)
        first(4, lambda i: (row(q), tip(i)))
        sweep1(q, wing, 4)
        sweep2(q, False)
    for u in range(2):
        copy_out(row(0), u, u).wait()
    for c in (*near_edge, *far_edge, *near_one, *near_zero, *far_one, *far_zero, desc_up, desc_dn, corner, relay_near, relay_far, relay_last, swap):
        c.wait_send()


def on_device(n, unary_cost, descriptors, valid_rows, offsets):
    data = jnp.transpose(unary_cost, (1, 0, 2, 3)) * valid_rows.astype(BF).T[:, :, None, None]
    hbm = pl.BlockSpec(memory_space=pl.ANY)
    e, disp = pl.pallas_call(
        functools.partial(kernel, n),
        in_specs=[hbm, hbm, pl.BlockSpec(memory_space=pltpu.VMEM)],
        out_specs=[hbm, pl.BlockSpec(memory_space=pltpu.VMEM)],
        out_shape=[jax.ShapeDtypeStruct((4, LAB, 4, COLS), F32), jax.ShapeDtypeStruct((2, 4, 4, COLS), F32)],
        scratch_shapes=[
            pltpu.VMEM((4, 12, LAB, COLS), BF),
            pltpu.VMEM((2, 8, LAB, COLS), BF),
            pltpu.VMEM((4, 12, LAB, COLS), BF),
            pltpu.VMEM((12, LAB, COLS), BF),
            pltpu.VMEM((4, 12, FEAT, COLS), BF),
            pltpu.VMEM((8, FEAT, COLS), BF),
            pltpu.VMEM((4, 8, FEAT, COLS), BF),
            pltpu.VMEM((4, 8, LAB, COLS), BF),
            pltpu.VMEM((12, LAB, FEAT), BF),
            pltpu.VMEM((12, FEAT, LAB), BF),
            pltpu.VMEM((LAB, LAB), BF),
            pltpu.VMEM((8, LAB), F32),
            pltpu.VMEM((LAB, COLS), BF),
            pltpu.VMEM((LAB, COLS), BF),
            pltpu.VMEM((FEAT, COLS), BF),
            pltpu.VMEM((FEAT, COLS), BF),
            pltpu.VMEM((2, LAB, COLS), F32),
            pltpu.SemaphoreType.DMA((19,)),
            pltpu.SemaphoreType.DMA((19,)),
            pltpu.SemaphoreType.DMA((2,)),
            pltpu.SemaphoreType.DMA((2,)),
        ],
        compiler_params=pltpu.CompilerParams(collective_id=0, has_side_effects=True, vmem_limit_bytes=67043328),
        name="mega",
    )(data, descriptors, offsets.T)
    return jnp.transpose(e, (0, 2, 1, 3)), disp


def solution(mesh):
    in_specs = (P("gz", "rows", None, None), P("gz", None, None), P("gz", "rows"), P())
    out_specs = (P("gz", "rows", None, None), P(None, "gz", "rows", None))
    return jax.shard_map(functools.partial(on_device, mesh.shape["gz"]), mesh=mesh, in_specs=in_specs, out_specs=out_specs, check_vma=False)
```
